32 devices in a mesh: tile: 8 (over y, x, core), coarse: 4 (over z).
Axes of the slice: x: 2, y: 2, z: 4, core: 2. Of those that a mesh axis runs over, the one named last changes fastest.
Arguments:
- features: bfloat16 [524288, 256], P(('tile', 'coarse')), may hold values from -6 to 6
- weight_in: bfloat16 [256, 256], replicated, may hold values from -0.375 to 0.375
- bias_in: float32 [256], replicated, may hold values from -3 to 3
- weight_mid: bfloat16 [256, 256], replicated, may hold values from -0.375 to 0.375
- bias_mid: float32 [256], replicated, may hold values from -3 to 3
- weight_out: float32 [256], replicated, may hold values from -0.375 to 0.375
- fine_block: int32 [32, 128], P(('tile', 'coarse')), may hold values from 0 to 127, each once within a row
- owner_dev: int32 [4096, 1], P(('tile', 'coarse')), may hold values from 0 to 31; in each aligned block of 128 rows (0 to 127, 128 to 255, ...) at most 8 rows name the same one
- coarse_local: int32 [4096], P(('tile', 'coarse')), may hold values from 0 to 127
- warp_weights: bfloat16 [4096, 128, 64], P(('tile', 'coarse')), may hold values from -0.5 to 0.5
- reference_map: float32 [64, 4096], P(None, ('tile', 'coarse')), may hold values from -6 to 6
- valid_mask: int32 [64, 4096], P(None, ('tile', 'coarse')), may hold values 0 or 1
Outputs:
- coarse_pred: float32 [64, 4096], P(None, ('tile', 'coarse'))
- grad_weight_in: float32 [256, 256], replicated
- grad_bias_in: float32 [256], replicated
- grad_weight_mid: float32 [256, 256], replicated
- grad_bias_mid: float32 [256], replicated
- grad_weight_out: float32 [256], replicated
The draws below stay inside these ranges and needn't reach their ends.
Inputs may be any that keep to these rules, and one draw needn't show every extreme that they name: `fine_block`: each row lists the device's 128 fine blocks once each. `owner_dev`: among the rows of one device no owner is named more than 8 times; some owner is named exactly 8 times by some device.
All inputs are finite; a program needn't handle non-finite values. No bound on the sum of `valid_mask` on one device may be relied on, other than what follows from the above.
Results may differ from the reference program's by a relative error of at most 0.0043.
Values sent between devices are 32-bit elements; how exact they have to be, the bound alone decides.
No kernel may reach another device: no remote copies, remote signals or barrier semaphores. Data moves between devices by JAX's collectives and lax.ppermute only.
A program may use at most 128 MiB of HBM per device.

```python
import math
import jax
import jax.numpy as jnp
import numpy as np
from jax import lax

C = 256
H = 256
PIX_BLOCK = 128
CELLS = 64
FB_DEV = 128
CB_DEV = 128
CAP = 8
NFB = 4096
NCB = 4096
DEVICES = 32


def place_ends(drawn, stream_key, low, high):
    dims = drawn.shape
    index_at = [jax.random.randint(jax.random.fold_in(stream_key, axis), (), 0, dims[axis]) for axis in range(len(dims))]
    drawn = drawn.at[tuple(index_at)].set(low)
    longest = dims.index(max(dims))
    index_at[longest] = (index_at[longest] + 1) % dims[longest]
    return drawn.at[tuple(index_at)].set(high)


def shard_levels(key, shape, pieces, least, high):
    factor_of, own = 1.0, jax.random.fold_in(key, 6)
    for dim, shards_of in pieces:
        steps = jnp.exp(jax.random.uniform(jax.random.fold_in(own, dim), (shards_of,), jnp.float32, least / len(pieces), high / len(pieces)))
        factor_of = factor_of * jnp.repeat(steps, shape[dim] // shards_of).reshape([-1 if axis == dim else 1 for axis in range(len(shape))])
    return factor_of


def routed_block(stream_key, own, number, rows, count, top, most, lean):
    ranking = jax.random.permutation(stream_key, count)
    crowded, ordinary = shares(count, rows * top, most, lean, True), shares(count, rows * top, most, lean, False)
    places = jnp.arange(count)

    def named(sizes, turn):
        used = int((sizes > 0).sum())
        fixed = max(1, used // 4)
        passed = fixed + (places - fixed + turn * (used - fixed)) % max(1, count - fixed)
        return jnp.zeros((count,), jnp.int32).at[ranking[jnp.where(places < fixed, places, passed)]].set(jnp.asarray(sizes, jnp.int32))

    sizes = jnp.where(number % 4 == 0, named(crowded, number // 4), named(ordinary, number - number // 4 - 1))
    mixed = jax.random.permutation(jax.random.fold_in(own, 3), count)
    source_of, taker = mixed[0:count // 2 * 2:2], mixed[1:count // 2 * 2:2]
    slack = jnp.minimum(sizes[source_of] - 1, most - sizes[taker]) // 2
    slack = jnp.where((source_of == ranking[0]) | (taker == ranking[0]) | (sizes[taker] == 0), 0, jnp.maximum(slack, 0))
    passed = jax.random.randint(jax.random.fold_in(own, 4), (count // 2,), 0, 1 << 20) % (slack + 1)
    sizes = sizes.at[source_of].add(-passed).at[taker].add(passed)
    labels = jnp.searchsorted(jnp.cumsum(sizes), jnp.arange(rows * top), side="right").astype(jnp.int32)
    listing = labels.reshape(top, rows).T
    listing = listing[jax.random.permutation(jax.random.fold_in(own, 1), rows)]
    turn = jax.random.randint(jax.random.fold_in(own, 2), (rows, 1), 0, top)
    return jnp.take_along_axis(listing, (jnp.arange(top)[None, :] + turn) % top, axis=1)


def shares(number_of, total, reach, skew, full):
    loads = [(1 << 20) // math.isqrt(grade ** skew) + 1 for grade in range(1, number_of + 1)]
    largest = reach if full else min(reach, max(-(-total // number_of), total * loads[0] // sum(loads)))
    least = 1 if total - largest >= number_of - 1 else 0
    given, surplus = [largest] + [least] * (number_of - 1), total - largest - least * (number_of - 1)
    while surplus > 0:
        candidates = [i for i in range(1, number_of) if given[i] < largest] or [i for i in range(1, number_of) if given[i] < reach]
        whole, left = sum([loads[i] for i in candidates]), surplus
        for i in candidates:
            more = min(reach - given[i], max(1, left * loads[i] // whole), surplus)
            given[i] = given[i] + more
            surplus = surplus - more
    return np.array(given)


def bell_draw(key, shape, spread, bound, pieces=(), held_as=jnp.bfloat16):
    array = spread * jax.random.normal(key, shape, jnp.float32)
    if pieces:
        array = array * shard_levels(key, shape, pieces, -0.22, 0.18)
    return jnp.clip(array, -bound, bound).astype(held_as)


def setup_inputs(seed: int = 0) -> dict:
    arg_keys = jax.random.split(jax.random.key(seed), 13)
    features = bell_draw(arg_keys[0], (NFB * PIX_BLOCK, C), 1.0, 6.0, ((0, 32),))
    weight_in = bell_draw(arg_keys[1], (C, H), C ** -0.5, 0.375)
    bias_in = bell_draw(arg_keys[2], (H,), 0.5, 3.0, (), jnp.float32)
    weight_mid = bell_draw(arg_keys[3], (H, H), H ** -0.5, 0.375)
    bias_mid = bell_draw(arg_keys[4], (H,), 0.5, 3.0, (), jnp.float32)
    weight_out = bell_draw(arg_keys[5], (H,), H ** -0.5, 0.375, (), jnp.float32)
    fine_block = jax.vmap(lambda own: jax.random.permutation(own, FB_DEV))(jax.random.split(arg_keys[6], DEVICES)).reshape((DEVICES, FB_DEV)).astype(jnp.int32)
    owner_dev_keys = jax.random.split(jax.random.fold_in(arg_keys[7], 1), NFB // FB_DEV)
    owner_dev_turns = jax.random.permutation(jax.random.fold_in(arg_keys[7], 3), NFB // FB_DEV)
    owner_dev = jax.vmap(lambda own, number: routed_block(jax.random.fold_in(arg_keys[7], 2), own, number, FB_DEV, DEVICES, 1, CAP, 2))(owner_dev_keys, owner_dev_turns).reshape((NFB, 1))
    coarse_local = place_ends(jax.random.randint(arg_keys[8], (NFB,), 0, CB_DEV), jax.random.fold_in(arg_keys[8], 1), 0, CB_DEV - 1).astype(jnp.int32)
    warp_weights = bell_draw(arg_keys[9], (NFB, PIX_BLOCK, CELLS), PIX_BLOCK ** -0.5, 0.5, ((0, 32),))
    reference_map = bell_draw(arg_keys[10], (CELLS, NCB), 1.0, 6.0, ((1, 32),), jnp.float32)
    valid_mask = place_ends((jax.random.randint(arg_keys[11], (CELLS, NCB), 0, 4) < 3).astype(jnp.int32), jax.random.fold_in(arg_keys[11], 1), 0, 1)
    return {"features": features, "weight_in": weight_in, "bias_in": bias_in, "weight_mid": weight_mid, "bias_mid": bias_mid, "weight_out": weight_out, "fine_block": fine_block, "owner_dev": owner_dev, "coarse_local": coarse_local, "warp_weights": warp_weights, "reference_map": reference_map, "valid_mask": valid_mask}


def run_head(pixel_feats, weight_in, bias_in, weight_mid, bias_mid, weight_out):
    pre_first = jnp.dot(pixel_feats, weight_in, preferred_element_type=jnp.float32) + bias_in
    act_first = jnp.maximum(pre_first, 0.0).astype(jnp.bfloat16)
    pre_second = jnp.dot(act_first, weight_mid, preferred_element_type=jnp.float32) + bias_mid
    act_second = jnp.maximum(pre_second, 0.0)
    predicted = jnp.dot(act_second, weight_out, precision=lax.Precision.HIGHEST)
    return (pre_first, act_first, pre_second, act_second, predicted)

def reference(features, weight_in, bias_in, weight_mid, bias_mid, weight_out, fine_block, owner_dev, coarse_local, warp_weights, reference_map, valid_mask):
    feat_dev = features.reshape(DEVICES, FB_DEV * PIX_BLOCK, C)
    warp_dev = warp_weights.reshape(DEVICES, FB_DEV, PIX_BLOCK, CELLS)

    def forward(packed):
        pixel_feats, block_list, warp_list = packed
        predicted = run_head(pixel_feats, weight_in, bias_in, weight_mid, bias_mid, weight_out)[4]
        chosen = predicted.reshape(FB_DEV, PIX_BLOCK)[block_list]
        return jnp.einsum('kp,kpc->kc', chosen, warp_list.astype(jnp.float32), precision=lax.Precision.HIGHEST)
    partial_value = lax.map(forward, (feat_dev, fine_block, warp_dev)).reshape(FB_DEV * DEVICES, CELLS)
    gid = (owner_dev[:, 0] * CB_DEV + coarse_local).astype(jnp.int32)
    coarse_pred = jnp.zeros((CELLS, CB_DEV * DEVICES), jnp.float32).at[:, gid].add(partial_value.T)
    loss_scale = 1.0 / math.sqrt(FB_DEV * DEVICES * PIX_BLOCK)
    grad_coarse = loss_scale * valid_mask.astype(jnp.float32) * (coarse_pred - reference_map)
    grad_cols = grad_coarse[:, gid].T.reshape(DEVICES, FB_DEV, CELLS)

    def backward(carry, packed):
        pixel_feats, block_list, warp_list, col_list = packed
        pre_first, act_first, pre_second, act_second, predicted = run_head(pixel_feats, weight_in, bias_in, weight_mid, bias_mid, weight_out)
        grad_blocks = jnp.einsum('kpc,kc->kp', warp_list.astype(jnp.float32), col_list, precision=lax.Precision.HIGHEST)
        grad_pred = jnp.zeros((FB_DEV, PIX_BLOCK), jnp.float32).at[block_list].set(grad_blocks).reshape(-1)
        gw_out = lax.optimization_barrier(jnp.sum(act_second * grad_pred[:, None], axis=0))
        grad_pre2 = grad_pred[:, None] * weight_out[None, :] * (pre_second > 0).astype(jnp.float32)
        gb_mid = lax.optimization_barrier(jnp.sum(grad_pre2, axis=0))
        grad_low2 = grad_pre2.astype(jnp.bfloat16)
        gw_mid = jnp.dot(act_first.T, grad_low2, preferred_element_type=jnp.float32)
        grad_act1 = jnp.dot(grad_low2, weight_mid.T, preferred_element_type=jnp.float32)
        grad_low1 = (grad_act1 * (pre_first > 0).astype(jnp.float32)).astype(jnp.bfloat16)
        gb_in = lax.optimization_barrier(jnp.sum(lax.optimization_barrier(grad_low1).astype(jnp.float32), axis=0))
        gw_in = jnp.dot(pixel_feats.T, grad_low1, preferred_element_type=jnp.float32)
        return ((carry[0] + gw_in, carry[1] + gb_in, carry[2] + gw_mid, carry[3] + gb_mid, carry[4] + gw_out), None)
    start = (jnp.zeros((C, H), jnp.float32), jnp.zeros((H,), jnp.float32), jnp.zeros((H, H), jnp.float32), jnp.zeros((H,), jnp.float32), jnp.zeros((H,), jnp.float32))
    totals, _ = lax.scan(backward, start, (feat_dev, fine_block, warp_dev, grad_cols))
    return (coarse_pred, totals[0], totals[1], totals[2], totals[3], totals[4])
```

```python
import functools
import math

import jax
import jax.numpy as jnp
from jax import lax
from jax.experimental import pallas as pl
from jax.experimental.pallas import tpu as pltpu
from jax.sharding import Mesh
from jax.sharding import PartitionSpec as P

ALL = ("chip", "core", "coarse")
CHIPS = ("chip", "coarse")
F32 = jnp.float32
BF16 = jnp.bfloat16
NT = (((1,), (1,)), ((), ()))
NN = (((1,), (0,)), ((), ()))


def dot(a, b, dims=NN):
    return lax.dot_general(a, b, dims, preferred_element_type=F32)


def split3(x):
    hi = x.astype(BF16).astype(F32)
    rest = x - hi
    mid = rest.astype(BF16).astype(F32)
    low = (rest - mid).astype(BF16).astype(F32)
    return hi, mid, low


def terms_by_row(x):
    hi, mid, low = split3(x)
    row = lax.broadcasted_iota(jnp.int32, x.shape, 0)
    return jnp.where(row == 0, hi, jnp.where(row == 1, mid, jnp.where(row == 2, low, 0.0)))


def column(vec, lanes):
    return jnp.broadcast_to(vec, (lanes, vec.shape[1])).T


def head_kernel(
    devices, cap, chunk,
    fine_s, owner_s, local_s,
    feat_r, win_r, bin_r, wmid_r, bmid_r, wout_r, warp_r,
    act1_r, act2_r, send_r, rows_r,
    winT, wmidT, b1, b2, wo, pred8, count_s,
):
    step = pl.program_id(0)
    blocks, cells, pix = warp_r.shape
    tile = feat_r.shape[0]
    per_chunk = chunk // pix

    @pl.when(step == 0)
    def _():
        winT[...] = win_r[...].astype(F32).T.astype(BF16)
        wmidT[...] = wmid_r[...].astype(F32).T.astype(BF16)
        b1[...] = column(bin_r[...], chunk)
        b2[...] = column(bmid_r[...], chunk)
        wo[...] = column(wout_r[...], chunk)
        lane = lax.broadcasted_iota(jnp.int32, send_r.shape, 1)
        send_r[...] = jnp.where(lane < cells, 0.0, -1.0)

        def clear(i, c):
            count_s[i] = 0
            return c

        lax.fori_loop(0, devices, clear, 0)

        def slot(k, c):
            owner = owner_s[k]
            rank = count_s[owner]
            count_s[owner] = rank + 1
            rows_r[k] = owner * cap + rank
            return c

        lax.fori_loop(0, blocks, slot, 0)

    for i in range(tile // chunk):
        here = slice(i * chunk, (i + 1) * chunk)
        pre1 = dot(winT[...], feat_r[here, :], NT) + b1[...]
        act1 = jnp.maximum(pre1, 0.0).astype(BF16)
        act1_r[0, :, here] = act1
        act2 = jnp.maximum(dot(wmidT[...], act1) + b2[...], 0.0)
        act2_r[0, :, here] = act2.astype(BF16)
        pred = jnp.sum(act2 * wo[...], axis=0, keepdims=True)
        for b in range(per_chunk):
            one = jnp.broadcast_to(pred[:, b * pix:(b + 1) * pix], (8, pix))
            pred8[step * (tile // pix) + i * per_chunk + b] = terms_by_row(one)

    @pl.when(step == pl.num_programs(0) - 1)
    def _():
        def entry(k, c):
            part = dot(pred8[fine_s[k]].astype(BF16), warp_r[k], NT)
            part = jnp.sum(part, axis=0, keepdims=True)
            row = rows_r[k]
            send_r[pl.ds(row, 1), 0:cells] = part
            tag = jnp.full((1, send_r.shape[1] - cells), local_s[k], jnp.int32).astype(F32)
            send_r[pl.ds(row, 1), cells:] = tag
            return c

        lax.fori_loop(0, blocks, entry, 0, unroll=8)


def coarse_kernel(scale, recv_r, ref_r, valid_r, cp_r, back_r):
    cells, cb = ref_r.shape
    recv = recv_r[...]
    lane = lax.broadcasted_iota(jnp.int32, recv.shape, 1)
    half = recv.shape[1] // 2
    tag = jnp.where(lane < half, pltpu.roll(recv, half, 1), recv)
    pick = (tag == lane.astype(F32)).astype(F32).astype(BF16)
    vals = recv.T[0:cells, :]
    three = jnp.concatenate([t.astype(BF16) for t in split3(vals)], axis=0)
    sums = dot(three, pick)
    cp = sums[0:cells] + sums[cells:2 * cells] + sums[2 * cells:3 * cells]
    cp_r[...] = cp
    grad = scale * valid_r[...].astype(F32) * (cp - ref_r[...])
    wide = jnp.concatenate([t.astype(BF16) for t in split3(grad)], axis=1)
    wide = jnp.concatenate([wide, jnp.zeros_like(wide)], axis=0)
    back_r[...] = dot(jnp.concatenate([pick, pick, pick], axis=1), wide, NT)


def back_kernel(
    chunk,
    fine_s, rows_s,
    ret_r, warp_r, feat_r, act1_r, act2_r, wmid_r, wout_r,
    out_r,
    wo, grad_s, gl1_s, gl2_s, acc_mid, acc_in, acc_wo, acc_bm, acc_bi,
):
    step = pl.program_id(0)
    blocks, cells, pix = warp_r.shape
    hidden, tile = act1_r.shape[1:]
    per_chunk = chunk // pix

    @pl.when(step == 0)
    def _():
        wo[...] = column(wout_r[...], chunk)
        for acc in (acc_mid, acc_in, acc_wo, acc_bm, acc_bi):
            acc[...] = jnp.zeros_like(acc)

        def entry(k, c):
            row = jnp.broadcast_to(ret_r[pl.ds(rows_s[k], 1), :], (8, ret_r.shape[1]))
            terms = terms_by_row(row)[:, 0:cells].astype(BF16)
            grad = jnp.sum(dot(terms, warp_r[k]), axis=0, keepdims=True)
            grad_s[pl.ds(fine_s[k], 1), :] = grad
            return c

        lax.fori_loop(0, blocks, entry, 0, unroll=8)

    for i in range(tile // chunk):
        here = slice(i * chunk, (i + 1) * chunk)
        first = step * (tile // pix) + i * per_chunk
        grad = jnp.concatenate([grad_s[pl.ds(first + b, 1), :] for b in range(per_chunk)], axis=1)
        act2 = act2_r[0, :, here].astype(F32)
        on = act2 > 0
        gp2 = jnp.where(on, grad * wo[...], 0.0)
        gl2 = gp2.astype(BF16)
        gl2_s[:, here] = gl2
        gwo = act2 * grad
        low1 = jnp.where(act1_r[0, :, here].astype(F32) > 0, dot(wmid_r[...], gl2), 0.0)
        gl1_s[:, here] = low1.astype(BF16)
        for acc, val in ((acc_wo, gwo), (acc_bm, gp2), (acc_bi, low1)):
            total = val[:, 0:pix]
            for b in range(1, per_chunk):
                total = total + val[:, b * pix:(b + 1) * pix]
            acc[...] += total
    acc_mid[...] += dot(act1_r[0], gl2_s[...], NT)
    acc_in[...] += dot(gl1_s[...], feat_r[...])

    @pl.when(step == pl.num_programs(0) - 1)
    def _():
        def as_row(acc):
            return jnp.sum(acc[...].T, axis=0, keepdims=True)

        width = acc_mid.shape[1]
        zero = jnp.zeros((6, width), F32)
        tail_mid = jnp.concatenate([as_row(acc_bm), as_row(acc_wo), zero], axis=0)
        tail_in = jnp.concatenate([as_row(acc_bi), jnp.zeros((1, width), F32), zero], axis=0)
        base = 0
        for acc, tail in ((acc_mid, tail_mid), (acc_in, tail_in)):
            for lanes in range(0, width, 128):
                out_r[base:base + hidden, :] = acc[:, lanes:lanes + 128]
                out_r[base + hidden:base + hidden + 8, :] = tail[:, lanes:lanes + 128]
                base += hidden + 8


def last_kernel(core_s, mine_r, other_r, gwin_r, gbin_r, gwmid_r, gbmid_r, gwout_r):
    hidden = gwmid_r.shape[0]
    first = core_s[0] == 0

    def part(want_first):
        use_mine = jnp.logical_xor(first, not want_first)
        whole = jnp.where(use_mine, mine_r[...], other_r[...])
        pieces, tails = [], []
        for base in range(0, whole.shape[0], hidden + 8):
            pieces.append(whole[base:base + hidden])
            tails.append(whole[base + hidden:base + hidden + 8])
        return jnp.concatenate(pieces, axis=1), jnp.concatenate(tails, axis=1)

    mid, tail = part(True)
    gwmid_r[...] = mid
    gbmid_r[...] = tail[0:1]
    gwout_r[...] = tail[1:2]
    win, tail = part(False)
    gwin_r[...] = win.T
    gbin_r[...] = tail[0:1]


def vmem():
    return pl.BlockSpec(memory_space=pltpu.VMEM)


def smem():
    return pl.BlockSpec(memory_space=pltpu.SMEM)


def fixed(shape):
    return pl.BlockSpec(shape, lambda i: (0,) * len(shape), pipeline_mode=pl.Buffered(1))


def all_to_all(x, axes):
    return lax.all_to_all(x, axes, split_axis=0, concat_axis=0, tiled=True)


def shards(
    features, weight_in, bias_in, weight_mid, bias_mid, weight_out,
    fine_block, owner_dev, coarse_local, warp_weights, reference_map, valid_mask,
):
    blocks, pix, cells = warp_weights.shape
    pixels, chans = features.shape
    hidden = weight_mid.shape[0]
    cb = reference_map.shape[1]
    devices = lax.axis_size(ALL)
    chips = lax.axis_size(CHIPS)
    cap = max(2, 2 * blocks // devices)
    slots = devices * cap
    tile, chunk = 2048, 256
    steps = pixels // tile

    warp = jnp.swapaxes(warp_weights, 1, 2)
    fine = fine_block[0]
    owner = owner_dev[:, 0]
    row = lambda v: v[None, :]

    act1, act2, send, rows = pl.pallas_call(
        functools.partial(head_kernel, devices, cap, chunk),
        grid=(steps,),
        in_specs=[
            smem(), smem(), smem(),
            pl.BlockSpec((tile, chans), lambda i: (i, 0)),
            fixed((chans, hidden)), fixed((1, hidden)), fixed((hidden, hidden)),
            fixed((1, hidden)), fixed((1, hidden)), fixed((blocks, cells, pix)),
        ],
        out_specs=[
            pl.BlockSpec((1, hidden, tile), lambda i: (i, 0, 0)),
            pl.BlockSpec((1, hidden, tile), lambda i: (i, 0, 0)),
            pl.BlockSpec((slots, 2 * cells), lambda i: (0, 0)),
            smem(),
        ],
        out_shape=[
            jax.ShapeDtypeStruct((steps, hidden, tile), BF16),
            jax.ShapeDtypeStruct((steps, hidden, tile), BF16),
            jax.ShapeDtypeStruct((slots, 2 * cells), F32),
            jax.ShapeDtypeStruct((blocks,), jnp.int32),
        ],
        scratch_shapes=[
            pltpu.VMEM((hidden, chans), BF16),
            pltpu.VMEM((hidden, hidden), BF16),
            pltpu.VMEM((hidden, chunk), F32),
            pltpu.VMEM((hidden, chunk), F32),
            pltpu.VMEM((hidden, chunk), F32),
            pltpu.VMEM((blocks, 8, pix), F32),
            pltpu.SMEM((devices,), jnp.int32),
        ],
        name="head",
    )(fine, owner, coarse_local, features, weight_in, row(bias_in), weight_mid, row(bias_mid),
      row(weight_out), warp)

    recv = all_to_all(send.reshape(devices, cap, 2 * cells), ALL).reshape(slots, 2 * cells)

    scale = 1.0 / math.sqrt(blocks * devices * pix)
    coarse_pred, back = pl.pallas_call(
        functools.partial(coarse_kernel, scale),
        in_specs=[vmem()] * 3,
        out_specs=[vmem()] * 2,
        out_shape=[
            jax.ShapeDtypeStruct((cells, cb), F32),
            jax.ShapeDtypeStruct((slots, 2 * cells), F32),
        ],
        name="coarse",
    )(recv, reference_map, valid_mask)

    returned = all_to_all(back.reshape(devices, cap, 2 * cells), ALL).reshape(slots, 2 * cells)

    packed_rows = 2 * (hidden + 8) * (chans // 128)
    packed = pl.pallas_call(
        functools.partial(back_kernel, chunk),
        grid=(steps,),
        in_specs=[
            smem(), smem(),
            fixed((slots, 2 * cells)), fixed((blocks, cells, pix)),
            pl.BlockSpec((tile, chans), lambda i: (i, 0)),
            pl.BlockSpec((1, hidden, tile), lambda i: (i, 0, 0)),
            pl.BlockSpec((1, hidden, tile), lambda i: (i, 0, 0)),
            fixed((hidden, hidden)), fixed((1, hidden)),
        ],
        out_specs=pl.BlockSpec((packed_rows, 128), lambda i: (0, 0)),
        out_shape=jax.ShapeDtypeStruct((packed_rows, 128), F32),
        scratch_shapes=[
            pltpu.VMEM((hidden, chunk), F32),
            pltpu.VMEM((blocks, pix), F32),
            pltpu.VMEM((hidden, tile), BF16),
            pltpu.VMEM((hidden, tile), BF16),
            pltpu.VMEM((hidden, hidden), F32),
            pltpu.VMEM((hidden, chans), F32),
            pltpu.VMEM((hidden, pix), F32),
            pltpu.VMEM((hidden, pix), F32),
            pltpu.VMEM((hidden, pix), F32),
        ],
        name="back",
    )(fine, rows, returned, warp, features, act1, act2, weight_mid, row(weight_out))

    core = lax.axis_index("core")
    run = packed_rows * 128 // 2 // chips
    halves = packed.reshape(2, chips, 1, run)
    swap = [(0, 1), (1, 0)]
    keep = lax.dynamic_index_in_dim(halves, core, 0, False)
    give = lax.dynamic_index_in_dim(halves, 1 - core, 0, False)
    half = keep + lax.ppermute(give, "core", swap)
    share = jnp.sum(all_to_all(half, CHIPS), axis=0)
    mine = all_to_all(jnp.broadcast_to(share[None], (chips, 1, run)), CHIPS)
    other = lax.ppermute(mine, "core", swap)

    flat = lambda x: x.reshape(packed_rows // 2, 128)
    gw_in, gb_in, gw_mid, gb_mid, gw_out = pl.pallas_call(
        last_kernel,
        in_specs=[smem(), vmem(), vmem()],
        out_specs=[vmem()] * 5,
        out_shape=[
            jax.ShapeDtypeStruct((chans, hidden), F32),
            jax.ShapeDtypeStruct((1, hidden), F32),
            jax.ShapeDtypeStruct((hidden, hidden), F32),
            jax.ShapeDtypeStruct((1, hidden), F32),
            jax.ShapeDtypeStruct((1, hidden), F32),
        ],
        name="last",
    )(core.astype(jnp.int32).reshape(1), flat(mine), flat(other))
    return (coarse_pred, gw_in, gb_in[0], gw_mid, gb_mid[0], gw_out[0])


def solution(mesh):
    tile, coarse = mesh.shape["tile"], mesh.shape["coarse"]
    split = Mesh(mesh.devices.reshape(tile // 2, 2, coarse), ALL)
    in_specs = (
        P(ALL, None), P(), P(), P(), P(), P(),
        P(ALL, None), P(ALL, None), P(ALL), P(ALL, None, None), P(None, ALL), P(None, ALL),
    )
    out_specs = (P(None, ALL), P(), P(), P(), P(), P())
    return jax.shard_map(shards, mesh=split, in_specs=in_specs, out_specs=out_specs, check_vma=False)
```

```python
import functools
import math

import jax
import jax.numpy as jnp
from jax import lax
from jax.experimental import pallas as pl
from jax.experimental.pallas import tpu as pltpu
from jax.sharding import Mesh
from jax.sharding import PartitionSpec as P

ALL = ("chip", "core", "coarse")
CHIPS = ("chip", "coarse")
F32 = jnp.float32
BF16 = jnp.bfloat16
NT = (((1,), (1,)), ((), ()))
NN = (((1,), (0,)), ((), ()))


def dot(a, b, dims=NN):
    return lax.dot_general(a, b, dims, preferred_element_type=F32)


def split3(x):
    hi = x.astype(BF16).astype(F32)
    rest = x - hi
    mid = rest.astype(BF16).astype(F32)
    low = (rest - mid).astype(BF16).astype(F32)
    return hi, mid, low


def terms_by_row(x):
    hi, mid, low = split3(x)
    row = lax.broadcasted_iota(jnp.int32, x.shape, 0)
    return jnp.where(row == 0, hi, jnp.where(row == 1, mid, jnp.where(row == 2, low, 0.0)))


def column(vec, lanes):
    return jnp.broadcast_to(vec, (lanes, vec.shape[1])).T


def widen(col, lanes):
    return jnp.concatenate([col] * (lanes // col.shape[1]), axis=1)


def head_kernel(
    devices, cap, chunk,
    fine_s, owner_s, local_s,
    feat_h, win_r, bin_r, wmid_r, bmid_r, wout_r, warp_r,
    act1_h, act2_h, send_r, rows_r, inv_r,
    feat_v, act1_v, act2_v, winT, wmidT, b1, b2, wo, part_s, count_s, sem_in, sem_out,
):
    blocks, cells, pix = warp_r.shape
    steps, tile = feat_v.shape[:2]
    per_chunk, per_step = chunk // pix, tile // pix

    def load(step):
        rows = pl.ds(pl.multiple_of(step * tile, tile), tile)
        return pltpu.make_async_copy(feat_h.at[rows], feat_v.at[step], sem_in.at[step])

    def stores(step):
        return [
            pltpu.make_async_copy(src.at[step], dst.at[step], sem_out.at[n, step])
            for n, (src, dst) in enumerate(((act1_v, act1_h), (act2_v, act2_h)))
        ]

    for step in range(steps):
        load(step).start()

    def prepare():
        winT[...] = win_r[...].astype(F32).T.astype(BF16)
        wmidT[...] = wmid_r[...].astype(F32).T.astype(BF16)
        b1[...] = column(bin_r[...], pix)
        b2[...] = column(bmid_r[...], pix)
        wo[...] = column(wout_r[...], pix)
        lane = lax.broadcasted_iota(jnp.int32, send_r.shape, 1)
        send_r[...] = jnp.where(lane < cells, 0.0, -1.0)
        for i in range(devices):
            count_s[i] = 0

        def invert(k, c):
            inv_r[fine_s[k]] = k
            return c

        lax.fori_loop(0, blocks, invert, 0, unroll=16)

    prepare()
    lax.fori_loop(0, steps, functools.partial(
        head_step, chunk, per_chunk, per_step, cap, load, stores,
        fine_s, owner_s, local_s, feat_v, act1_v, act2_v, warp_r,
        rows_r, inv_r, winT, wmidT, b1, b2, wo, part_s, count_s), 0)

    def place(k, c):
        send_r[pl.ds(rows_r[k], 1), :] = part_s[pl.ds(k, 1), :]
        return c

    lax.fori_loop(0, blocks, place, 0, unroll=16)
    for step in range(steps):
        for copy in stores(step):
            copy.wait()


def head_step(
    chunk, per_chunk, per_step, cap, load, stores,
    fine_s, owner_s, local_s, feat_v, act1_v, act2_v, warp_r,
    rows_r, inv_r, winT, wmidT, b1, b2, wo, part_s, count_s,
    step, carry,
):
    cells, pix = warp_r.shape[1:]
    tile = feat_v.shape[1]
    load(step).wait()
    feat_r, act1_r, act2_r = feat_v.at[step], act1_v.at[step], act2_v.at[step]

    for q in range(per_step):
        k = step * per_step + q
        owner = owner_s[k]
        rank = count_s[owner]
        count_s[owner] = rank + 1
        rows_r[k] = owner * cap + rank

    count = tile // chunk
    first, preds = {}, {}
    for i in range(count + 2):
        if i < count:
            here = slice(i * chunk, (i + 1) * chunk)
            pre1 = dot(winT[...], feat_r[here, :], NT) + widen(b1[...], chunk)
            first[i] = jnp.maximum(pre1.astype(BF16), jnp.zeros((), BF16))
            act1_r[:, here] = first[i]
        if 0 <= i - 1 < count:
            here = slice((i - 1) * chunk, i * chunk)
            pre2 = dot(wmidT[...], first.pop(i - 1)) + widen(b2[...], chunk)
            act2_r[:, here] = pre2.astype(BF16)
            kept = jnp.maximum(pre2, 0.0) * widen(wo[...], chunk)
            preds[i - 1] = jnp.sum(kept, axis=0, keepdims=True)
        if i >= 2:
            pred = preds.pop(i - 2)
            for b in range(per_chunk):
                k = inv_r[step * per_step + (i - 2) * per_chunk + b]
                one = jnp.broadcast_to(pred[:, b * pix:(b + 1) * pix], (8, pix))
                part = dot(terms_by_row(one).astype(BF16), warp_r[k], NT)
                part_s[pl.ds(k, 1), 0:cells] = jnp.sum(part, axis=0, keepdims=True)
                tag = jnp.full((1, part_s.shape[1] - cells), local_s[k], jnp.int32).astype(F32)
                part_s[pl.ds(k, 1), cells:] = tag

    for copy in stores(step):
        copy.start()
    return carry


def gate_kernel(begin, *refs):
    act1_h, act2_h, wmid_r, wout_r = refs[:4]
    unit_h, token_r, act1_v, act2_v, unit_v, mixed, sem_in, sem_out = refs[-8:]
    count = unit_v.shape[0]

    def loads(i):
        return [
            pltpu.make_async_copy(src.at[begin + i], dst.at[i], sem_in.at[n, i])
            for n, (src, dst) in enumerate(((act2_h, act2_v), (act1_h, act1_v)))
        ]

    def store(i):
        return pltpu.make_async_copy(unit_v.at[i], unit_h.at[begin + i], sem_out.at[i])

    for i in range(count):
        for copy in loads(i):
            copy.start()
    mixed[...] = (wmid_r[...].astype(F32) * wout_r[...]).astype(BF16)
    token_r[...] = jnp.zeros_like(token_r)

    def one(i, carry):
        for copy in loads(i):
            copy.wait()
        for at in range(0, act2_v.shape[2], 256):
            here = slice(at, at + 256)
            on = act2_v[i, :, here] > 0
            mask = jnp.where(on, jnp.ones((), BF16), jnp.zeros((), BF16))
            unit = dot(mixed[...], mask).astype(BF16)
            unit_v[i, :, here] = jnp.where(act1_v[i, :, here] > 0, unit, jnp.zeros((), BF16))
        store(i).start()
        return carry

    lax.fori_loop(0, count, one, 0)
    for i in range(count):
        store(i).wait()


def coarse_kernel(scale, recv_r, ref_r, valid_r, token_r, cp_r, back_r):
    cells, cb = ref_r.shape
    recv = recv_r[...]
    lane = lax.broadcasted_iota(jnp.int32, recv.shape, 1)
    half = recv.shape[1] // 2
    tag = jnp.where(lane < half, pltpu.roll(recv, half, 1), recv)
    pick = (tag == lane.astype(F32)).astype(F32).astype(BF16)
    vals = recv.T[0:cells, :]
    three = jnp.concatenate([t.astype(BF16) for t in split3(vals)], axis=0)
    sums = dot(three, pick)
    cp = sums[0:cells] + sums[cells:2 * cells] + sums[2 * cells:3 * cells]
    cp_r[...] = cp
    grad = scale * valid_r[...].astype(F32) * (cp - ref_r[...])
    wide = jnp.concatenate([t.astype(BF16) for t in split3(grad)], axis=1)
    wide = jnp.concatenate([wide, jnp.zeros_like(wide)], axis=0)
    back_r[...] = dot(jnp.concatenate([pick, pick, pick], axis=1), wide, NT)


def back_kernel(
    chunk,
    rows_s, inv_s,
    core_s, ret_r, warp_r, feat_h, act1_h, act2_h, unit_h,
    keep_r, give_r,
    feat_v, act1_v, act2_v, unit_v, grad_s, gated_s, low1_s, acc_mid, acc_in, acc_bi, sem,
):
    blocks, cells, pix = warp_r.shape
    steps, hidden, tile = act1_v.shape
    per_chunk, per_step = chunk // pix, tile // pix

    def loads(step):
        rows = pl.ds(pl.multiple_of(step * tile, tile), tile)
        pairs = ((act2_h.at[step], act2_v), (act1_h.at[step], act1_v),
                 (unit_h.at[step], unit_v), (feat_h.at[rows], feat_v))
        return [
            pltpu.make_async_copy(src, dst.at[step], sem.at[n, step])
            for n, (src, dst) in enumerate(pairs)
        ]

    for step in range(steps):
        for copy in loads(step):
            copy.start()

    def entry(of_step, q):
        k = inv_s[jnp.minimum(of_step * per_step + q, blocks - 1)]
        row = jnp.broadcast_to(ret_r[pl.ds(rows_s[k], 1), :], (8, ret_r.shape[1]))
        terms = terms_by_row(row)[:, 0:cells].astype(BF16)
        grad_s[q:q + 1, :] = jnp.sum(dot(terms, warp_r[k]), axis=0, keepdims=True)

    for acc in (acc_mid, acc_in, acc_bi):
        acc[...] = jnp.zeros_like(acc)
    for q in range(per_step):
        entry(0, q)

    def one(step, carry):
        for copy in loads(step):
            copy.wait()
        grads = grad_s[...]

        def scale(i):
            here = slice(i * chunk, (i + 1) * chunk)
            first = i * per_chunk
            grad = jnp.concatenate(
                [grads[first + b:first + b + 1] for b in range(per_chunk)], axis=1)
            short = jnp.broadcast_to(grad.astype(BF16), (hidden, chunk))
            gated_s[:, here] = jnp.where(act2_v[step, :, here] > 0, short, jnp.zeros((), BF16))
            low1_s[:, here] = (unit_v[step, :, here].astype(F32) * grad).astype(BF16)

        def gather(i):
            here = slice(i * chunk, (i + 1) * chunk)
            ones = jnp.ones((16, chunk), BF16)
            lhs = jnp.concatenate([act1_v[step, :, here], ones], axis=0)
            acc_mid[...] += dot(lhs, gated_s[:, here], NT)
            acc_in[...] += dot(low1_s[:, here], feat_v[step, here, :])
            acc_bi[...] += dot(ones, low1_s[:, here], NT)

        count = tile // chunk
        scale(0)
        for i in range(count):
            for b in range(per_chunk):
                entry(step + 1, i * per_chunk + b)
            if i + 1 < count:
                scale(i + 1)
            gather(i)
        return carry

    lax.fori_loop(0, steps, one, 0)

    width = acc_mid.shape[1]
    first = core_s[0] == 0
    halves = ((acc_mid, acc_mid[hidden:hidden + 8, :]), (acc_in, acc_bi[0:8, :]))
    for n, (acc, tail) in enumerate(halves):
        mine = first if n == 0 else jnp.logical_not(first)
        for out, chosen in ((keep_r, mine), (give_r, jnp.logical_not(mine))):
            @pl.when(chosen)
            def _(acc=acc, tail=tail, out=out):
                base = 0
                for lanes in range(0, width, 128):
                    out[base:base + hidden, :] = acc[0:hidden, lanes:lanes + 128]
                    out[base + hidden:base + hidden + 8, :] = tail[:, lanes:lanes + 128]
                    base += hidden + 8


def last_kernel(
    core_s, mine_r, other_r, wmid_r, bmid_r, wout_r,
    gwin_r, gbin_r, gwmid_r, gbmid_r, gwout_r,
):
    hidden = gwmid_r.shape[0]
    first = core_s[0] == 0

    def part(want_first):
        use_mine = jnp.logical_xor(first, not want_first)
        whole = jnp.where(use_mine, mine_r[...], other_r[...])
        pieces, tails = [], []
        for base in range(0, whole.shape[0], hidden + 8):
            pieces.append(whole[base:base + hidden])
            tails.append(whole[base + hidden:base + hidden + 8])
        return jnp.concatenate(pieces, axis=1), jnp.concatenate(tails, axis=1)

    gated, tail = part(True)
    count = tail[0:1]
    gwmid_r[...] = gated * wout_r[...]
    gbmid_r[...] = count * wout_r[...]
    through = jnp.sum(gated * wmid_r[...].astype(F32), axis=0, keepdims=True)
    gwout_r[...] = through + bmid_r[...] * count
    win, tail = part(False)
    gwin_r[...] = win.T
    gbin_r[...] = tail[0:1]


def vmem():
    return pl.BlockSpec(memory_space=pltpu.VMEM)


def smem():
    return pl.BlockSpec(memory_space=pltpu.SMEM)


def limit(mebibytes):
    return pltpu.CompilerParams(vmem_limit_bytes=mebibytes << 20)


def hbm():
    return pl.BlockSpec(memory_space=pl.ANY)


def all_to_all(x, axes):
    return lax.all_to_all(x, axes, split_axis=0, concat_axis=0, tiled=True)


def shards(
    features, weight_in, bias_in, weight_mid, bias_mid, weight_out,
    fine_block, owner_dev, coarse_local, warp_weights, reference_map, valid_mask,
):
    blocks, pix, cells = warp_weights.shape
    pixels, chans = features.shape
    hidden = weight_mid.shape[0]
    cb = reference_map.shape[1]
    devices = lax.axis_size(ALL)
    chips = lax.axis_size(CHIPS)
    cap = max(2, 2 * blocks // devices)
    slots = devices * cap
    tile, chunk = 2048, 512
    steps = pixels // tile

    warp = jnp.swapaxes(warp_weights, 1, 2)
    fine = fine_block[0]
    owner = owner_dev[:, 0]
    row = lambda v: v[None, :]

    act_shape = jax.ShapeDtypeStruct((steps, hidden, tile), BF16)
    act_v = pltpu.VMEM((steps, hidden, tile), BF16)
    feat_v = pltpu.VMEM((steps, tile, chans), BF16)
    act1, act2, send, rows, inv = pl.pallas_call(
        functools.partial(head_kernel, devices, cap, chunk),
        in_specs=[smem()] * 3 + [hbm()] + [vmem()] * 6,
        out_specs=[hbm(), hbm(), vmem(), smem(), smem()],
        out_shape=[
            act_shape, act_shape,
            jax.ShapeDtypeStruct((slots, 2 * cells), F32),
            jax.ShapeDtypeStruct((blocks,), jnp.int32),
            jax.ShapeDtypeStruct((blocks,), jnp.int32),
        ],
        scratch_shapes=[
            feat_v, act_v, act_v,
            pltpu.VMEM((hidden, chans), BF16),
            pltpu.VMEM((hidden, hidden), BF16),
            pltpu.VMEM((hidden, pix), F32),
            pltpu.VMEM((hidden, pix), F32),
            pltpu.VMEM((hidden, pix), F32),
            pltpu.VMEM((blocks, 2 * cells), F32),
            pltpu.SMEM((devices,), jnp.int32),
            pltpu.SemaphoreType.DMA((steps,)),
            pltpu.SemaphoreType.DMA((2, steps)),
        ],
        compiler_params=limit(58),
        name="head",
    )(fine, owner, coarse_local, features, weight_in, row(bias_in), weight_mid, row(bias_mid),
      row(weight_out), warp)

    def unit_part(begin, count, *after):
        part_v = pltpu.VMEM((count, hidden, tile), BF16)
        return pl.pallas_call(
            functools.partial(gate_kernel, begin),
            in_specs=[hbm(), hbm(), vmem(), vmem()] + [hbm()] * len(after),
            out_specs=[hbm(), vmem()],
            out_shape=[act_shape, jax.ShapeDtypeStruct((8, 128), F32)],
            scratch_shapes=[
                part_v, part_v, part_v,
                pltpu.VMEM((hidden, hidden), BF16),
                pltpu.SemaphoreType.DMA((2, count)),
                pltpu.SemaphoreType.DMA((count,)),
            ],
            input_output_aliases={4: 0} if after else {},
            compiler_params=limit(58),
            cost_estimate=pl.CostEstimate(
                flops=2 * hidden * hidden * tile * count,
                bytes_accessed=6 * hidden * tile * count,
                transcendentals=0,
            ),
            name="gate",
        )(act1, act2, weight_mid, row(weight_out), *after)

    unit, token = unit_part(0, steps // 2)

    recv = all_to_all(send.reshape(devices, cap, 2 * cells), ALL).reshape(slots, 2 * cells)

    scale = 1.0 / math.sqrt(blocks * devices * pix)
    coarse_pred, back = pl.pallas_call(
        functools.partial(coarse_kernel, scale),
        in_specs=[vmem()] * 4,
        out_specs=[vmem()] * 2,
        out_shape=[
            jax.ShapeDtypeStruct((cells, cb), F32),
            jax.ShapeDtypeStruct((slots, 2 * cells), F32),
        ],
        compiler_params=limit(4),
        name="coarse",
    )(recv, reference_map, valid_mask, token)

    unit, _ = unit_part(steps // 2, steps - steps // 2, unit, back)
    returned = all_to_all(back.reshape(devices, cap, 2 * cells), ALL).reshape(slots, 2 * cells)

    half_rows = (hidden + 8) * (chans // 128)
    half_shape = jax.ShapeDtypeStruct((half_rows, 128), F32)
    core = lax.axis_index("core").astype(jnp.int32).reshape(1)
    keep, give = pl.pallas_call(
        functools.partial(back_kernel, chunk),
        in_specs=[smem()] * 3 + [vmem(), vmem()] + [hbm()] * 4,
        out_specs=[vmem(), vmem()],
        out_shape=[half_shape, half_shape],
        scratch_shapes=[
            feat_v, act_v, act_v, act_v,
            pltpu.VMEM((tile // pix, pix), F32),
            pltpu.VMEM((hidden, tile), BF16),
            pltpu.VMEM((hidden, tile), BF16),
            pltpu.VMEM((hidden + 16, hidden), F32),
            pltpu.VMEM((hidden, chans), F32),
            pltpu.VMEM((16, hidden), F32),
            pltpu.SemaphoreType.DMA((4, steps)),
        ],
        compiler_params=limit(58),
        name="back",
    )(rows, inv, core, returned, warp, features, act1, act2, unit)

    run = half_rows * 128 // chips
    swap = [(0, 1), (1, 0)]
    half = keep.reshape(chips, 1, run) + lax.ppermute(give.reshape(chips, 1, run), "core", swap)
    share = jnp.sum(all_to_all(half, CHIPS), axis=0)
    mine = all_to_all(jnp.broadcast_to(share[None], (chips, 1, run)), CHIPS)
    other = lax.ppermute(mine, "core", swap)

    flat = lambda x: x.reshape(half_rows, 128)
    gw_in, gb_in, gw_mid, gb_mid, gw_out = pl.pallas_call(
        last_kernel,
        in_specs=[smem()] + [vmem()] * 5,
        out_specs=[vmem()] * 5,
        out_shape=[
            jax.ShapeDtypeStruct((chans, hidden), F32),
            jax.ShapeDtypeStruct((1, hidden), F32),
            jax.ShapeDtypeStruct((hidden, hidden), F32),
            jax.ShapeDtypeStruct((1, hidden), F32),
            jax.ShapeDtypeStruct((1, hidden), F32),
        ],
        compiler_params=limit(8),
        name="last",
    )(core, flat(mine), flat(other), weight_mid, row(bias_mid),
      row(weight_out))
    return (coarse_pred, gw_in, gb_in[0], gw_mid, gb_mid[0], gw_out[0])


def solution(mesh):
    tile, coarse = mesh.shape["tile"], mesh.shape["coarse"]
    split = Mesh(mesh.devices.reshape(tile // 2, 2, coarse), ALL)
    in_specs = (
        P(ALL, None), P(), P(), P(), P(), P(),
        P(ALL, None), P(ALL, None), P(ALL), P(ALL, None, None), P(None, ALL), P(None, ALL),
    )
    out_specs = (P(None, ALL), P(), P(), P(), P(), P())
    return jax.shard_map(shards, mesh=split, in_specs=in_specs, out_specs=out_specs, check_vma=False)
```

```python
import functools
import math

import jax
import jax.numpy as jnp
from jax import lax
from jax.experimental import pallas as pl
from jax.experimental.pallas import tpu as pltpu
from jax.sharding import Mesh
from jax.sharding import PartitionSpec as P

ALL = ("chip", "core", "coarse")
CHIPS = ("chip", "coarse")
F32 = jnp.float32
BF16 = jnp.bfloat16
F8 = jnp.float8_e4m3fn
NT = (((1,), (1,)), ((), ()))
NN = (((1,), (0,)), ((), ()))


def dot(a, b, dims=NN):
    return lax.dot_general(a, b, dims, preferred_element_type=F32)


def split3(x):
    hi = x.astype(BF16).astype(F32)
    rest = x - hi
    mid = rest.astype(BF16).astype(F32)
    low = (rest - mid).astype(BF16).astype(F32)
    return hi, mid, low


def terms_by_row(x):
    hi, mid, low = split3(x)
    row = lax.broadcasted_iota(jnp.int32, x.shape, 0)
    return jnp.where(row == 0, hi, jnp.where(row == 1, mid, jnp.where(row == 2, low, 0.0)))


def column(vec, lanes):
    return jnp.broadcast_to(vec, (lanes, vec.shape[1])).T


def widen(col, lanes):
    return jnp.concatenate([col] * (lanes // col.shape[1]), axis=1)


def head_kernel(
    devices, cap, chunk,
    fine_s, owner_s, local_s,
    feat_h, win_r, bin_r, wmid_r, bmid_r, wout_r, warp_r,
    act1_h, act2_h, send_r, rows_r, inv_r,
    feat_v, act1_v, act2_v, winT, wmidT, b1, b2, wo, part_s, count_s, sem_in, sem_out,
):
    blocks, cells, pix = warp_r.shape
    steps, tile = feat_v.shape[:2]
    per_chunk, per_step = chunk // pix, tile // pix

    def load(step):
        rows = pl.ds(pl.multiple_of(step * tile, tile), tile)
        return pltpu.make_async_copy(feat_h.at[rows], feat_v.at[step], sem_in.at[step])

    def stores(step):
        return [
            pltpu.make_async_copy(src.at[step], dst.at[step], sem_out.at[n, step])
            for n, (src, dst) in enumerate(((act1_v, act1_h), (act2_v, act2_h)))
        ]

    for step in range(steps):
        load(step).start()

    def prepare():
        winT[...] = win_r[...].astype(F32).T.astype(BF16)
        wmidT[...] = wmid_r[...].astype(F32).T.astype(BF16)
        b1[...] = column(bin_r[...], pix)
        b2[...] = column(bmid_r[...], pix)
        wo[...] = column(wout_r[...], pix)
        lane = lax.broadcasted_iota(jnp.int32, send_r.shape, 1)
        send_r[...] = jnp.where(lane < cells, 0.0, -1.0)
        for i in range(devices):
            count_s[i] = 0

        def invert(k, c):
            inv_r[fine_s[k]] = k
            return c

        lax.fori_loop(0, blocks, invert, 0, unroll=16)

    prepare()
    lax.fori_loop(0, steps, functools.partial(
        head_step, chunk, per_chunk, per_step, cap, load, stores,
        fine_s, owner_s, local_s, feat_v, act1_v, act2_v, warp_r,
        rows_r, inv_r, winT, wmidT, b1, b2, wo, part_s, count_s), 0)

    def place(k, c):
        send_r[pl.ds(rows_r[k], 1), :] = part_s[pl.ds(k, 1), :]
        return c

    lax.fori_loop(0, blocks, place, 0, unroll=16)
    for step in range(steps):
        for copy in stores(step):
            copy.wait()


def head_step(
    chunk, per_chunk, per_step, cap, load, stores,
    fine_s, owner_s, local_s, feat_v, act1_v, act2_v, warp_r,
    rows_r, inv_r, winT, wmidT, b1, b2, wo, part_s, count_s,
    step, carry,
):
    cells, pix = warp_r.shape[1:]
    tile = feat_v.shape[1]
    load(step).wait()
    feat_r, act1_r, act2_r = feat_v.at[step], act1_v.at[step], act2_v.at[step]

    for q in range(per_step):
        k = step * per_step + q
        owner = owner_s[k]
        rank = count_s[owner]
        count_s[owner] = rank + 1
        rows_r[k] = owner * cap + rank

    count = tile // chunk
    first, preds = {}, {}
    for i in range(count + 2):
        if i < count:
            here = slice(i * chunk, (i + 1) * chunk)
            pre1 = dot(winT[...], feat_r[here, :], NT) + widen(b1[...], chunk)
            first[i] = jnp.maximum(pre1.astype(BF16), jnp.zeros((), BF16))
            act1_r[:, here] = first[i]
        if 0 <= i - 1 < count:
            here = slice((i - 1) * chunk, i * chunk)
            pre2 = dot(wmidT[...], first.pop(i - 1)) + widen(b2[...], chunk)
            on = pre2.astype(BF16) > 0
            act2_r[:, here] = jnp.where(on, jnp.ones((), BF16), jnp.zeros((), BF16)).astype(F8)
            kept = jnp.maximum(pre2, 0.0) * widen(wo[...], chunk)
            preds[i - 1] = jnp.sum(kept, axis=0, keepdims=True)
        if i >= 2:
            pred = preds.pop(i - 2)
            for b in range(per_chunk):
                k = inv_r[step * per_step + (i - 2) * per_chunk + b]
                one = jnp.broadcast_to(pred[:, b * pix:(b + 1) * pix], (8, pix))
                part = dot(terms_by_row(one).astype(BF16), warp_r[k], NT)
                part_s[pl.ds(k, 1), 0:cells] = jnp.sum(part, axis=0, keepdims=True)
                tag = jnp.full((1, part_s.shape[1] - cells), local_s[k], jnp.int32).astype(F32)
                part_s[pl.ds(k, 1), cells:] = tag

    for copy in stores(step):
        copy.start()
    return carry


def gate_kernel(begin, *refs):
    act2_h, wmid_r, wout_r = refs[:3]
    unit_h, act2_v, unit_v, mixed, sem_in, sem_out = refs[-6:]
    count = unit_v.shape[0]

    def load(i):
        return pltpu.make_async_copy(act2_h.at[begin + i], act2_v.at[i], sem_in.at[i])

    def store(i):
        return pltpu.make_async_copy(unit_v.at[i], unit_h.at[begin + i], sem_out.at[i])

    for i in range(count):
        load(i).start()
    mixed[...] = (wmid_r[...].astype(F32) * wout_r[...]).astype(BF16)

    def one(i, carry):
        load(i).wait()
        for at in range(0, act2_v.shape[2], 256):
            here = slice(at, at + 256)
            mask = act2_v[i, :, here].astype(BF16)
            unit_v[i, :, here] = dot(mixed[...], mask).astype(BF16)
        store(i).start()
        return carry

    lax.fori_loop(0, count, one, 0)
    for i in range(count):
        store(i).wait()


def coarse_kernel(scale, recv_r, ref_r, valid_r, unit_h, cp_r, back_r):
    cells, cb = ref_r.shape
    recv = recv_r[...]
    lane = lax.broadcasted_iota(jnp.int32, recv.shape, 1)
    half = recv.shape[1] // 2
    tag = jnp.where(lane < half, pltpu.roll(recv, half, 1), recv)
    pick = (tag == lane.astype(F32)).astype(F32).astype(BF16)
    vals = recv.T[0:cells, :]
    three = jnp.concatenate([t.astype(BF16) for t in split3(vals)], axis=0)
    sums = dot(three, pick)
    cp = sums[0:cells] + sums[cells:2 * cells] + sums[2 * cells:3 * cells]
    cp_r[...] = cp
    grad = scale * valid_r[...].astype(F32) * (cp - ref_r[...])
    wide = jnp.concatenate([t.astype(BF16) for t in split3(grad)], axis=1)
    wide = jnp.concatenate([wide, jnp.zeros_like(wide)], axis=0)
    back_r[...] = dot(jnp.concatenate([pick, pick, pick], axis=1), wide, NT)


def back_kernel(
    chunk,
    rows_s, inv_s,
    core_s, ret_r, warp_r, feat_h, act1_h, act2_h, unit_h,
    keep_r, give_r,
    feat_v, act1_v, act2_v, unit_v, grad_s, gated_s, low1_s, acc_mid, acc_in, acc_bi, sem,
):
    blocks, cells, pix = warp_r.shape
    steps, hidden, tile = act1_v.shape
    per_chunk, per_step = chunk // pix, tile // pix

    def loads(step):
        rows = pl.ds(pl.multiple_of(step * tile, tile), tile)
        pairs = ((act2_h.at[step], act2_v), (act1_h.at[step], act1_v),
                 (unit_h.at[step], unit_v), (feat_h.at[rows], feat_v))
        return [
            pltpu.make_async_copy(src, dst.at[step], sem.at[n, step])
            for n, (src, dst) in enumerate(pairs)
        ]

    for step in range(steps):
        for copy in loads(step):
            copy.start()

    def entry(of_step, q):
        k = inv_s[jnp.minimum(of_step * per_step + q, blocks - 1)]
        row = jnp.broadcast_to(ret_r[pl.ds(rows_s[k], 1), :], (8, ret_r.shape[1]))
        terms = terms_by_row(row)[:, 0:cells].astype(BF16)
        grad_s[q:q + 1, :] = jnp.sum(dot(terms, warp_r[k]), axis=0, keepdims=True)

    for acc in (acc_mid, acc_in, acc_bi):
        acc[...] = jnp.zeros_like(acc)
    for q in range(per_step):
        entry(0, q)

    def one(step, carry):
        for copy in loads(step):
            copy.wait()
        grads = grad_s[...]

        def scale(i):
            here = slice(i * chunk, (i + 1) * chunk)
            first = i * per_chunk
            grad = jnp.concatenate(
                [grads[first + b:first + b + 1] for b in range(per_chunk)], axis=1)
            short = jnp.broadcast_to(grad.astype(BF16), (hidden, chunk))
            gated_s[:, here] = act2_v[step, :, here].astype(BF16) * short
            low1 = unit_v[step, :, here] * short
            low1 = jnp.where(act1_v[step, :, here] > 0, low1, jnp.zeros((), BF16))
            low1_s[:, here] = low1
            total = low1[:, 0:pix].astype(F32)
            for b in range(1, per_chunk):
                total = total + low1[:, b * pix:(b + 1) * pix].astype(F32)
            acc_bi[...] += total

        def gather(i):
            here = slice(i * chunk, (i + 1) * chunk)
            ones = jnp.ones((16, chunk), BF16)
            lhs = jnp.concatenate([act1_v[step, :, here], ones], axis=0)
            acc_mid[...] += dot(lhs, gated_s[:, here], NT)
            acc_in[...] += dot(low1_s[:, here], feat_v[step, here, :])

        count = tile // chunk
        scale(0)
        for i in range(count):
            for b in range(per_chunk):
                entry(step + 1, i * per_chunk + b)
            if i + 1 < count:
                scale(i + 1)
            gather(i)
        return carry

    lax.fori_loop(0, steps, one, 0)

    width = acc_mid.shape[1]
    first = core_s[0] == 0
    row_bi = jnp.sum(acc_bi[...].T, axis=0, keepdims=True)
    tail_in = jnp.concatenate([row_bi, jnp.zeros((7, width), F32)], axis=0)
    halves = ((acc_mid, acc_mid[hidden:hidden + 8, :]), (acc_in, tail_in))
    for n, (acc, tail) in enumerate(halves):
        mine = first if n == 0 else jnp.logical_not(first)
        for out, chosen in ((keep_r, mine), (give_r, jnp.logical_not(mine))):
            @pl.when(chosen)
            def _(acc=acc, tail=tail, out=out):
                base = 0
                for lanes in range(0, width, 128):
                    out[base:base + hidden, :] = acc[0:hidden, lanes:lanes + 128]
                    out[base + hidden:base + hidden + 8, :] = tail[:, lanes:lanes + 128]
                    base += hidden + 8


def last_kernel(
    core_s, mine_r, other_r, wmid_r, bmid_r, wout_r,
    gwin_r, gbin_r, gwmid_r, gbmid_r, gwout_r,
):
    hidden = gwmid_r.shape[0]
    first = core_s[0] == 0

    def part(want_first):
        use_mine = jnp.logical_xor(first, not want_first)
        whole = jnp.where(use_mine, mine_r[...], other_r[...])
        pieces, tails = [], []
        for base in range(0, whole.shape[0], hidden + 8):
            pieces.append(whole[base:base + hidden])
            tails.append(whole[base + hidden:base + hidden + 8])
        return jnp.concatenate(pieces, axis=1), jnp.concatenate(tails, axis=1)

    gated, tail = part(True)
    count = tail[0:1]
    gwmid_r[...] = gated * wout_r[...]
    gbmid_r[...] = count * wout_r[...]
    through = jnp.sum(gated * wmid_r[...].astype(F32), axis=0, keepdims=True)
    gwout_r[...] = through + bmid_r[...] * count
    win, tail = part(False)
    gwin_r[...] = win.T
    gbin_r[...] = tail[0:1]


def vmem():
    return pl.BlockSpec(memory_space=pltpu.VMEM)


def smem():
    return pl.BlockSpec(memory_space=pltpu.SMEM)


def limit(mebibytes):
    return pltpu.CompilerParams(vmem_limit_bytes=mebibytes << 20)


def hbm():
    return pl.BlockSpec(memory_space=pl.ANY)


def all_to_all(x, axes):
    return lax.all_to_all(x, axes, split_axis=0, concat_axis=0, tiled=True)


def shards(
    features, weight_in, bias_in, weight_mid, bias_mid, weight_out,
    fine_block, owner_dev, coarse_local, warp_weights, reference_map, valid_mask,
):
    blocks, pix, cells = warp_weights.shape
    pixels, chans = features.shape
    hidden = weight_mid.shape[0]
    cb = reference_map.shape[1]
    devices = lax.axis_size(ALL)
    chips = lax.axis_size(CHIPS)
    cap = max(2, 2 * blocks // devices)
    slots = devices * cap
    tile, chunk = 2048, 512
    steps = pixels // tile

    warp = jnp.swapaxes(warp_weights, 1, 2)
    fine = fine_block[0]
    owner = owner_dev[:, 0]
    row = lambda v: v[None, :]

    act_shape = jax.ShapeDtypeStruct((steps, hidden, tile), BF16)
    mask_shape = jax.ShapeDtypeStruct((steps, hidden, tile), F8)
    act_v = pltpu.VMEM((steps, hidden, tile), BF16)
    mask_v = pltpu.VMEM((steps, hidden, tile), F8)
    feat_v = pltpu.VMEM((steps, tile, chans), BF16)
    act1, act2, send, rows, inv = pl.pallas_call(
        functools.partial(head_kernel, devices, cap, 2 * chunk),
        in_specs=[smem()] * 3 + [hbm()] + [vmem()] * 6,
        out_specs=[hbm(), hbm(), vmem(), smem(), smem()],
        out_shape=[
            act_shape, mask_shape,
            jax.ShapeDtypeStruct((slots, 2 * cells), F32),
            jax.ShapeDtypeStruct((blocks,), jnp.int32),
            jax.ShapeDtypeStruct((blocks,), jnp.int32),
        ],
        scratch_shapes=[
            feat_v, act_v, mask_v,
            pltpu.VMEM((hidden, chans), BF16),
            pltpu.VMEM((hidden, hidden), BF16),
            pltpu.VMEM((hidden, pix), F32),
            pltpu.VMEM((hidden, pix), F32),
            pltpu.VMEM((hidden, pix), F32),
            pltpu.VMEM((blocks, 2 * cells), F32),
            pltpu.SMEM((devices,), jnp.int32),
            pltpu.SemaphoreType.DMA((steps,)),
            pltpu.SemaphoreType.DMA((2, steps)),
        ],
        compiler_params=limit(58),
        name="head",
    )(fine, owner, coarse_local, features, weight_in, row(bias_in), weight_mid, row(bias_mid),
      row(weight_out), warp)

    def unit_part(begin, count, *after):
        part_v = pltpu.VMEM((count, hidden, tile), BF16)
        return pl.pallas_call(
            functools.partial(gate_kernel, begin),
            in_specs=[hbm(), vmem(), vmem()] + [hbm()] * len(after),
            out_specs=hbm(),
            out_shape=act_shape,
            scratch_shapes=[
                pltpu.VMEM((count, hidden, tile), F8), part_v,
                pltpu.VMEM((hidden, hidden), BF16),
                pltpu.SemaphoreType.DMA((count,)),
                pltpu.SemaphoreType.DMA((count,)),
            ],
            input_output_aliases={3: 0} if after else {},
            compiler_params=limit(58),
            cost_estimate=pl.CostEstimate(
                flops=2 * hidden * hidden * tile * count,
                bytes_accessed=4 * hidden * tile * count,
                transcendentals=0,
            ),
            name="gate",
        )(act2, weight_mid, row(weight_out), *after)

    unit = unit_part(0, steps // 2)

    recv = all_to_all(send.reshape(devices, cap, 2 * cells), ALL).reshape(slots, 2 * cells)

    scale = 1.0 / math.sqrt(blocks * devices * pix)
    coarse_pred, back = pl.pallas_call(
        functools.partial(coarse_kernel, scale),
        in_specs=[vmem()] * 3 + [hbm()],
        out_specs=[vmem()] * 2,
        out_shape=[
            jax.ShapeDtypeStruct((cells, cb), F32),
            jax.ShapeDtypeStruct((slots, 2 * cells), F32),
        ],
        compiler_params=limit(48),
        name="coarse",
    )(recv, reference_map, valid_mask, unit)

    unit = unit_part(steps // 2, steps - steps // 2, unit, back)
    returned = all_to_all(back.reshape(devices, cap, 2 * cells), ALL).reshape(slots, 2 * cells)

    half_rows = (hidden + 8) * (chans // 128)
    half_shape = jax.ShapeDtypeStruct((half_rows, 128), F32)
    core = lax.axis_index("core").astype(jnp.int32).reshape(1)
    keep, give = pl.pallas_call(
        functools.partial(back_kernel, chunk),
        in_specs=[smem()] * 3 + [vmem(), vmem()] + [hbm()] * 4,
        out_specs=[vmem(), vmem()],
        out_shape=[half_shape, half_shape],
        scratch_shapes=[
            feat_v, act_v, mask_v, act_v,
            pltpu.VMEM((tile // pix, pix), F32),
            pltpu.VMEM((hidden, tile), BF16),
            pltpu.VMEM((hidden, tile), BF16),
            pltpu.VMEM((hidden + 16, hidden), F32),
            pltpu.VMEM((hidden, chans), F32),
            pltpu.VMEM((hidden, pix), F32),
            pltpu.SemaphoreType.DMA((4, steps)),
        ],
        compiler_params=limit(48),
        name="back",
    )(rows, inv, core, returned, warp, features, act1, act2, unit)

    run = half_rows * 128 // chips
    swap = [(0, 1), (1, 0)]
    half = keep.reshape(chips, 1, run) + lax.ppermute(give.reshape(chips, 1, run), "core", swap)
    share = jnp.sum(all_to_all(half, CHIPS), axis=0)
    mine = all_to_all(jnp.broadcast_to(share[None], (chips, 1, run)), CHIPS)
    other = lax.ppermute(mine, "core", swap)

    flat = lambda x: x.reshape(half_rows, 128)
    gw_in, gb_in, gw_mid, gb_mid, gw_out = pl.pallas_call(
        last_kernel,
        in_specs=[smem()] + [vmem()] * 5,
        out_specs=[vmem()] * 5,
        out_shape=[
            jax.ShapeDtypeStruct((chans, hidden), F32),
            jax.ShapeDtypeStruct((1, hidden), F32),
            jax.ShapeDtypeStruct((hidden, hidden), F32),
            jax.ShapeDtypeStruct((1, hidden), F32),
            jax.ShapeDtypeStruct((1, hidden), F32),
        ],
        compiler_params=limit(8),
        name="last",
    )(core, flat(mine), flat(other), weight_mid, row(bias_mid),
      row(weight_out))
    return (coarse_pred, gw_in, gb_in[0], gw_mid, gb_mid[0], gw_out[0])


def solution(mesh):
    tile, coarse = mesh.shape["tile"], mesh.shape["coarse"]
    split = Mesh(mesh.devices.reshape(tile // 2, 2, coarse), ALL)
    in_specs = (
        P(ALL, None), P(), P(), P(), P(), P(),
        P(ALL, None), P(ALL, None), P(ALL), P(ALL, None, None), P(None, ALL), P(None, ALL),
    )
    out_specs = (P(None, ALL), P(), P(), P(), P(), P())
    return jax.shard_map(shards, mesh=split, in_specs=in_specs, out_specs=out_specs, check_vma=False)
```

```python
import functools
import math

import jax
import jax.numpy as jnp
from jax import lax
from jax.experimental import pallas as pl
from jax.experimental.pallas import tpu as pltpu
from jax.sharding import Mesh
from jax.sharding import PartitionSpec as P

ALL = ("chip", "core", "coarse")
CHIPS = ("coarse", "chip")
EXCHANGE = ("coarse", "chip", "core")
F32 = jnp.float32
BF16 = jnp.bfloat16
F8 = jnp.float8_e4m3fn
NT = (((1,), (1,)), ((), ()))
NN = (((1,), (0,)), ((), ()))


def dot(a, b, dims=NN):
    return lax.dot_general(a, b, dims, preferred_element_type=F32)


def split3(x):
    hi = x.astype(BF16).astype(F32)
    rest = x - hi
    mid = rest.astype(BF16).astype(F32)
    low = (rest - mid).astype(BF16).astype(F32)
    return hi, mid, low


def terms_by_row(x):
    hi, mid, low = split3(x)
    row = lax.broadcasted_iota(jnp.int32, x.shape, 0)
    return jnp.where(row == 0, hi, jnp.where(row == 1, mid, jnp.where(row == 2, low, 0.0)))


def column(vec, lanes):
    return jnp.broadcast_to(vec, (lanes, vec.shape[1])).T


def widen(col, lanes):
    return jnp.concatenate([col] * (lanes // col.shape[1]), axis=1)


def head_kernel(
    devices, depth, cap, chunk,
    fine_s, owner_s, local_s,
    feat_h, win_r, bin_r, wmid_r, bmid_r, wout_r, warp_r,
    act1_h, act2_h, send_r, rows_r, inv_r,
    feat_v, act1_v, act2_v, winT, wmidT, b1, b2, wo, part_s, count_s, sem_in, sem_out,
):
    blocks, cells, pix = warp_r.shape
    steps, tile = feat_v.shape[:2]
    per_chunk, per_step = chunk // pix, tile // pix

    def load(step):
        rows = pl.ds(pl.multiple_of(step * tile, tile), tile)
        return pltpu.make_async_copy(feat_h.at[rows], feat_v.at[step], sem_in.at[step])

    def stores(step):
        return [
            pltpu.make_async_copy(src.at[step], dst.at[step], sem_out.at[n, step])
            for n, (src, dst) in enumerate(((act1_v, act1_h), (act2_v, act2_h)))
        ]

    for step in range(steps):
        load(step).start()

    def prepare():
        winT[...] = win_r[...].astype(F32).T.astype(BF16)
        wmidT[...] = wmid_r[...].astype(F32).T.astype(BF16)
        b1[...] = column(bin_r[...], pix)
        b2[...] = column(bmid_r[...], pix)
        wo[...] = column(wout_r[...], pix)
        lane = lax.broadcasted_iota(jnp.int32, send_r.shape, 2)
        send_r[...] = jnp.where(lane < cells, 0.0, -1.0)
        for i in range(devices):
            count_s[i] = 0

        def invert(k, c):
            inv_r[fine_s[k]] = k
            return c

        lax.fori_loop(0, blocks, invert, 0, unroll=16)

    prepare()
    lax.fori_loop(0, steps, functools.partial(
        head_step, chunk, per_chunk, per_step, (devices, depth, cap), load, stores,
        fine_s, owner_s, local_s, feat_v, act1_v, act2_v, warp_r,
        rows_r, inv_r, winT, wmidT, b1, b2, wo, part_s, count_s), 0)

    def place(k, c):
        send_r[rows_r[k]] = part_s[k]
        return c

    lax.fori_loop(0, blocks, place, 0, unroll=16)
    for step in range(steps):
        for copy in stores(step):
            copy.wait()


def head_step(
    chunk, per_chunk, per_step, sizes, load, stores,
    fine_s, owner_s, local_s, feat_v, act1_v, act2_v, warp_r,
    rows_r, inv_r, winT, wmidT, b1, b2, wo, part_s, count_s,
    step, carry,
):
    cells, pix = warp_r.shape[1:]
    tile = feat_v.shape[1]
    load(step).wait()
    feat_r, act1_r, act2_r = feat_v.at[step], act1_v.at[step], act2_v.at[step]

    for q in range(per_step):
        k = step * per_step + q
        owner = owner_s[k]
        rank = count_s[owner]
        count_s[owner] = rank + 1
        devices, depth, cap = sizes
        place = (owner % depth) * (devices // depth) + owner // depth
        rows_r[k] = place * cap + rank

    count = tile // chunk
    first, preds = {}, {}
    for i in range(count + 2):
        if i < count:
            here = slice(i * chunk, (i + 1) * chunk)
            pre1 = dot(winT[...], feat_r[here, :], NT) + widen(b1[...], chunk)
            first[i] = jnp.maximum(pre1.astype(BF16), jnp.zeros((), BF16))
            act1_r[:, here] = first[i]
        if 0 <= i - 1 < count:
            here = slice((i - 1) * chunk, i * chunk)
            pre2 = dot(wmidT[...], first.pop(i - 1)) + widen(b2[...], chunk)
            on = pre2.astype(BF16) > 0
            act2_r[:, here] = jnp.where(on, jnp.ones((), BF16), jnp.zeros((), BF16)).astype(F8)
            kept = jnp.maximum(pre2, 0.0) * widen(wo[...], chunk)
            preds[i - 1] = jnp.sum(kept, axis=0, keepdims=True)
        if i >= 2:
            pred = preds.pop(i - 2)
            for b in range(per_chunk):
                k = inv_r[step * per_step + (i - 2) * per_chunk + b]
                one = jnp.broadcast_to(pred[:, b * pix:(b + 1) * pix], (8, pix))
                part = dot(terms_by_row(one).astype(BF16), warp_r[k], NT)
                part_s[k, :, 0:cells] = jnp.sum(part, axis=0, keepdims=True)
                tag = jnp.full((1, part_s.shape[2] - cells), local_s[k], jnp.int32).astype(F32)
                part_s[k, :, cells:] = tag

    for copy in stores(step):
        copy.start()
    return carry


def gate_kernel(begin, *refs):
    act2_h, wmid_r, wout_r = refs[:3]
    unit_h, act2_v, unit_v, mixed, sem_in, sem_out = refs[-6:]
    count = unit_v.shape[0]

    def load(i):
        return pltpu.make_async_copy(act2_h.at[begin + i], act2_v.at[i], sem_in.at[i])

    def store(i):
        return pltpu.make_async_copy(unit_v.at[i], unit_h.at[begin + i], sem_out.at[i])

    for i in range(count):
        load(i).start()
    mixed[...] = (wmid_r[...].astype(F32) * wout_r[...]).astype(BF16)

    def one(i, carry):
        load(i).wait()
        for at in range(0, act2_v.shape[2], 256):
            here = slice(at, at + 256)
            mask = act2_v[i, :, here].astype(BF16)
            unit_v[i, :, here] = dot(mixed[...], mask).astype(BF16)
        store(i).start()
        return carry

    lax.fori_loop(0, count, one, 0)
    for i in range(count):
        store(i).wait()


def coarse_kernel(scale, recv_r, ref_r, valid_r, unit_h, cp_r, back_r):
    cells, cb = ref_r.shape
    recv = recv_r[...]
    lane = lax.broadcasted_iota(jnp.int32, recv.shape, 1)
    half = recv.shape[1] // 2
    tag = jnp.where(lane < half, pltpu.roll(recv, half, 1), recv)
    pick = (tag == lane.astype(F32)).astype(F32).astype(BF16)
    vals = recv.T[0:cells, :]
    three = jnp.concatenate([t.astype(BF16) for t in split3(vals)], axis=0)
    sums = dot(three, pick)
    cp = sums[0:cells] + sums[cells:2 * cells] + sums[2 * cells:3 * cells]
    cp_r[...] = cp
    grad = scale * valid_r[...].astype(F32) * (cp - ref_r[...])
    wide = jnp.concatenate([t.astype(BF16) for t in split3(grad)], axis=1)
    wide = jnp.concatenate([wide, jnp.zeros_like(wide)], axis=0)
    back_r[...] = dot(jnp.concatenate([pick, pick, pick], axis=1), wide, NT)


def back_kernel(
    chunk,
    rows_s, inv_s,
    core_s, ret_r, warp_r, feat_h, act1_h, act2_h, unit_h,
    keep_r, give_r,
    feat_v, act1_v, act2_v, unit_v, grad_s, gated_s, low1_s, acc_mid, acc_in, acc_bi, sem,
):
    blocks, cells, pix = warp_r.shape
    steps, hidden, tile = act1_v.shape
    per_chunk, per_step = chunk // pix, tile // pix

    def loads(step):
        rows = pl.ds(pl.multiple_of(step * tile, tile), tile)
        pairs = ((act2_h.at[step], act2_v), (act1_h.at[step], act1_v),
                 (unit_h.at[step], unit_v), (feat_h.at[rows], feat_v))
        return [
            pltpu.make_async_copy(src, dst.at[step], sem.at[n, step])
            for n, (src, dst) in enumerate(pairs)
        ]

    for step in range(steps):
        for copy in loads(step):
            copy.start()

    def entry(of_step, q):
        k = inv_s[jnp.minimum(of_step * per_step + q, blocks - 1)]
        row = jnp.broadcast_to(ret_r[pl.ds(rows_s[k], 1), :], (8, ret_r.shape[1]))
        terms = terms_by_row(row)[:, 0:cells].astype(BF16)
        grad_s[q:q + 1, :] = jnp.sum(dot(terms, warp_r[k]), axis=0, keepdims=True)

    for acc in (acc_mid, acc_in, acc_bi):
        acc[...] = jnp.zeros_like(acc)
    for q in range(per_step):
        entry(0, q)

    def one(step, carry):
        for copy in loads(step):
            copy.wait()
        grads = grad_s[...]

        def scale(i):
            here = slice(i * chunk, (i + 1) * chunk)
            first = i * per_chunk
            grad = jnp.concatenate(
                [grads[first + b:first + b + 1] for b in range(per_chunk)], axis=1)
            short = jnp.broadcast_to(grad.astype(BF16), (hidden, chunk))
            gated_s[:, here] = act2_v[step, :, here].astype(BF16) * short
            low1 = unit_v[step, :, here] * short
            low1 = jnp.where(act1_v[step, :, here] > 0, low1, jnp.zeros((), BF16))
            low1_s[:, here] = low1
            total = low1[:, 0:pix].astype(F32)
            for b in range(1, per_chunk):
                total = total + low1[:, b * pix:(b + 1) * pix].astype(F32)
            acc_bi[...] += total

        def gather(i):
            here = slice(i * chunk, (i + 1) * chunk)
            ones = jnp.ones((16, chunk), BF16)
            lhs = jnp.concatenate([act1_v[step, :, here], ones], axis=0)
            acc_mid[...] += dot(lhs, gated_s[:, here], NT)
            acc_in[...] += dot(low1_s[:, here], feat_v[step, here, :])

        count = tile // chunk
        scale(0)
        for i in range(count):
            for b in range(per_chunk):
                entry(step + 1, i * per_chunk + b)
            if i + 1 < count:
                scale(i + 1)
            gather(i)
        return carry

    lax.fori_loop(0, steps, one, 0)

    width = acc_mid.shape[1]
    first = core_s[0] == 0
    row_bi = jnp.sum(acc_bi[...].T, axis=0, keepdims=True)
    tail_in = jnp.concatenate([row_bi, jnp.zeros((7, width), F32)], axis=0)
    halves = ((acc_mid, acc_mid[hidden:hidden + 8, :]), (acc_in, tail_in))
    for n, (acc, tail) in enumerate(halves):
        mine = first if n == 0 else jnp.logical_not(first)
        for out, chosen in ((keep_r, mine), (give_r, jnp.logical_not(mine))):
            @pl.when(chosen)
            def _(acc=acc, tail=tail, out=out):
                base = 0
                for lanes in range(0, width, 128):
                    out[base:base + hidden, :] = acc[0:hidden, lanes:lanes + 128]
                    out[base + hidden:base + hidden + 8, :] = tail[:, lanes:lanes + 128]
                    base += hidden + 8


def last_kernel(
    core_s, mine_r, other_r, wmid_r, bmid_r, wout_r,
    gwin_r, gbin_r, gwmid_r, gbmid_r, gwout_r,
):
    hidden = gwmid_r.shape[0]
    first = core_s[0] == 0

    def part(want_first):
        use_mine = jnp.logical_xor(first, not want_first)
        whole = jnp.where(use_mine, mine_r[...], other_r[...])
        pieces, tails = [], []
        for base in range(0, whole.shape[0], hidden + 8):
            pieces.append(whole[base:base + hidden])
            tails.append(whole[base + hidden:base + hidden + 8])
        return jnp.concatenate(pieces, axis=1), jnp.concatenate(tails, axis=1)

    gated, tail = part(True)
    count = tail[0:1]
    gwmid_r[...] = gated * wout_r[...]
    gbmid_r[...] = count * wout_r[...]
    through = jnp.sum(gated * wmid_r[...].astype(F32), axis=0, keepdims=True)
    gwout_r[...] = through + bmid_r[...] * count
    win, tail = part(False)
    gwin_r[...] = win.T
    gbin_r[...] = tail[0:1]


def vmem():
    return pl.BlockSpec(memory_space=pltpu.VMEM)


def smem():
    return pl.BlockSpec(memory_space=pltpu.SMEM)


def limit(mebibytes):
    return pltpu.CompilerParams(vmem_limit_bytes=mebibytes << 20)


def hbm():
    return pl.BlockSpec(memory_space=pl.ANY)


def all_to_all(x, axes):
    return lax.all_to_all(x, axes, split_axis=0, concat_axis=0, tiled=True)


def shards(
    features, weight_in, bias_in, weight_mid, bias_mid, weight_out,
    fine_block, owner_dev, coarse_local, warp_weights, reference_map, valid_mask,
):
    blocks, pix, cells = warp_weights.shape
    pixels, chans = features.shape
    hidden = weight_mid.shape[0]
    cb = reference_map.shape[1]
    devices = lax.axis_size(ALL)
    chips = lax.axis_size(CHIPS)
    cap = max(2, 2 * blocks // devices)
    slots = devices * cap
    tile, chunk = 2048, 512
    steps = pixels // tile

    warp = jnp.swapaxes(warp_weights, 1, 2)
    fine = fine_block[0]
    owner = owner_dev[:, 0]
    row = lambda v: v[None, :]

    act_shape = jax.ShapeDtypeStruct((steps, hidden, tile), BF16)
    mask_shape = jax.ShapeDtypeStruct((steps, hidden, tile), F8)
    act_v = pltpu.VMEM((steps, hidden, tile), BF16)
    mask_v = pltpu.VMEM((steps, hidden, tile), F8)
    feat_v = pltpu.VMEM((steps, tile, chans), BF16)
    act1, act2, send, rows, inv = pl.pallas_call(
        functools.partial(head_kernel, devices, lax.axis_size("coarse"), cap, 2 * chunk),
        in_specs=[smem()] * 3 + [hbm()] + [vmem()] * 6,
        out_specs=[hbm(), hbm(), vmem(), smem(), smem()],
        out_shape=[
            act_shape, mask_shape,
            jax.ShapeDtypeStruct((slots, 1, 2 * cells), F32),
            jax.ShapeDtypeStruct((blocks,), jnp.int32),
            jax.ShapeDtypeStruct((blocks,), jnp.int32),
        ],
        scratch_shapes=[
            feat_v, act_v, mask_v,
            pltpu.VMEM((hidden, chans), BF16),
            pltpu.VMEM((hidden, hidden), BF16),
            pltpu.VMEM((hidden, pix), F32),
            pltpu.VMEM((hidden, pix), F32),
            pltpu.VMEM((hidden, pix), F32),
            pltpu.VMEM((blocks, 1, 2 * cells), F32),
            pltpu.SMEM((devices,), jnp.int32),
            pltpu.SemaphoreType.DMA((steps,)),
            pltpu.SemaphoreType.DMA((2, steps)),
        ],
        compiler_params=limit(58),
        name="head",
    )(fine, owner, coarse_local, features, weight_in, row(bias_in), weight_mid, row(bias_mid),
      row(weight_out), warp)

    def unit_part(begin, count, *after):
        part_v = pltpu.VMEM((count, hidden, tile), BF16)
        return pl.pallas_call(
            functools.partial(gate_kernel, begin),
            in_specs=[hbm(), vmem(), vmem()] + [hbm()] * len(after),
            out_specs=hbm(),
            out_shape=act_shape,
            scratch_shapes=[
                pltpu.VMEM((count, hidden, tile), F8), part_v,
                pltpu.VMEM((hidden, hidden), BF16),
                pltpu.SemaphoreType.DMA((count,)),
                pltpu.SemaphoreType.DMA((count,)),
            ],
            input_output_aliases={3: 0} if after else {},
            compiler_params=limit(58),
            cost_estimate=pl.CostEstimate(
                flops=2 * hidden * hidden * tile * count,
                bytes_accessed=4 * hidden * tile * count,
                transcendentals=0,
            ),
            name="gate",
        )(act2, weight_mid, row(weight_out), *after)

    unit = unit_part(0, steps // 2)

    recv = all_to_all(send.reshape(devices, cap, 2 * cells), EXCHANGE).reshape(slots, 2 * cells)

    scale = 1.0 / math.sqrt(blocks * devices * pix)
    coarse_pred, back = pl.pallas_call(
        functools.partial(coarse_kernel, scale),
        in_specs=[vmem()] * 3 + [hbm()],
        out_specs=[vmem()] * 2,
        out_shape=[
            jax.ShapeDtypeStruct((cells, cb), F32),
            jax.ShapeDtypeStruct((slots, 2 * cells), F32),
        ],
        compiler_params=limit(48),
        name="coarse",
    )(recv, reference_map, valid_mask, unit)

    unit = unit_part(steps // 2, steps - steps // 2, unit, back)
    returned = all_to_all(back.reshape(devices, cap, 2 * cells), EXCHANGE).reshape(slots, 2 * cells)

    half_rows = (hidden + 8) * (chans // 128)
    half_shape = jax.ShapeDtypeStruct((half_rows, 128), F32)
    core = lax.axis_index("core").astype(jnp.int32).reshape(1)
    keep, give = pl.pallas_call(
        functools.partial(back_kernel, chunk),
        in_specs=[smem()] * 3 + [vmem(), vmem()] + [hbm()] * 4,
        out_specs=[vmem(), vmem()],
        out_shape=[half_shape, half_shape],
        scratch_shapes=[
            feat_v, act_v, mask_v, act_v,
            pltpu.VMEM((tile // pix, pix), F32),
            pltpu.VMEM((hidden, tile), BF16),
            pltpu.VMEM((hidden, tile), BF16),
            pltpu.VMEM((hidden + 16, hidden), F32),
            pltpu.VMEM((hidden, chans), F32),
            pltpu.VMEM((hidden, pix), F32),
            pltpu.SemaphoreType.DMA((4, steps)),
        ],
        compiler_params=limit(48),
        name="back",
    )(rows, inv, core, returned, warp, features, act1, act2, unit)

    run = half_rows * 128 // chips
    swap = [(0, 1), (1, 0)]
    half = keep.reshape(chips, 1, run) + lax.ppermute(give.reshape(chips, 1, run), "core", swap)
    share = jnp.sum(all_to_all(half, CHIPS), axis=0)
    mine = all_to_all(jnp.broadcast_to(share[None], (chips, 1, run)), CHIPS)
    other = lax.ppermute(mine, "core", swap)

    flat = lambda x: x.reshape(half_rows, 128)
    gw_in, gb_in, gw_mid, gb_mid, gw_out = pl.pallas_call(
        last_kernel,
        in_specs=[smem()] + [vmem()] * 5,
        out_specs=[vmem()] * 5,
        out_shape=[
            jax.ShapeDtypeStruct((chans, hidden), F32),
            jax.ShapeDtypeStruct((1, hidden), F32),
            jax.ShapeDtypeStruct((hidden, hidden), F32),
            jax.ShapeDtypeStruct((1, hidden), F32),
            jax.ShapeDtypeStruct((1, hidden), F32),
        ],
        compiler_params=limit(8),
        name="last",
    )(core, flat(mine), flat(other), weight_mid, row(bias_mid),
      row(weight_out))
    return (coarse_pred, gw_in, gb_in[0], gw_mid, gb_mid[0], gw_out[0])


def solution(mesh):
    tile, coarse = mesh.shape["tile"], mesh.shape["coarse"]
    split = Mesh(mesh.devices.reshape(tile // 2, 2, coarse), ALL)
    in_specs = (
        P(ALL, None), P(), P(), P(), P(), P(),
        P(ALL, None), P(ALL, None), P(ALL), P(ALL, None, None), P(None, ALL), P(None, ALL),
    )
    out_specs = (P(None, ALL), P(), P(), P(), P(), P())
    return jax.shard_map(shards, mesh=split, in_specs=in_specs, out_specs=out_specs, check_vma=False)
```
